256 devices in a mesh: ctx: 64 (over z, x, core), exp: 4 (over y).
Axes of the slice: x: 4, y: 4, z: 8, core: 2. Of those that a mesh axis runs over, the one named last changes fastest.
Arguments:
- tokens: bfloat16 [32768, 2048], P(('ctx', 'exp')), may hold values from -6 to 6
- norm_gain: float32 [2048], replicated, may hold values from 0.1 to 1.9
- w_query: bfloat16 [2048, 2048], P(None, 'exp'), may hold values from -0.125 to 0.125
- w_key: bfloat16 [2048, 2048], P(None, 'exp'), may hold values from -0.125 to 0.125
- w_value: bfloat16 [2048, 2048], P(None, 'exp'), may hold values from -0.125 to 0.125
- head_gain: float32 [2048], P('exp'), may hold values from 0.1 to 1.9
- w_out: bfloat16 [2048, 2048], P('exp'), may hold values from -0.125 to 0.125
- ffn_gain: float32 [2048], replicated, may hold values from 0.1 to 1.9
- indices: int32 [32768, 2], P(('ctx', 'exp')), may hold values from 0 to 63, all different within a row; in each aligned block of 128 rows (0 to 127, 128 to 255, ...) at most 5 rows name the same one
- gates: bfloat16 [32768, 2], P(('ctx', 'exp')), may hold values from 0.049804688 to 1
- w_gate: bfloat16 [64, 2048, 1024], P('ctx', None, 'exp'), may hold values from -0.125 to 0.125
- w_up: bfloat16 [64, 2048, 1024], P('ctx', None, 'exp'), may hold values from -0.125 to 0.125
- w_down: bfloat16 [64, 2048, 1024], P('ctx', None, 'exp'), may hold values from -0.1875 to 0.1875
Outputs:
- mixed: bfloat16 [32768, 2048], P(('ctx', 'exp'))
The draws below stay inside these ranges and needn't reach their ends.
Inputs may be any that keep to these rules, and one draw needn't show every extreme that they name: `indices`: the two entries of a row differ. In the rows of one device no expert is named more than 5 times, and in some device's rows some expert is named exactly 5 times.
All inputs are finite; a program needn't handle non-finite values.
Results may differ from the reference program's by a relative error of at most 0.015.
Values may be sent and summed in bfloat16 or wider, within the bound.
A program may use at most 128 MiB of HBM per device.

```python
import math
from functools import partial
import jax
import jax.numpy as jnp
import numpy as np
from jax import lax

D = 2048
H = 16
HD = 128
FF_E = 1024
BLK = 512
TOK_DEV = 128
EXPERTS = 64
TOKENS = 32768
CAP = 5
N_EXP = 4


def level_of(stream_key, dims, cuts, smallest, top_value):
    def one(dim, blocks):
        steps = jax.random.uniform(jax.random.fold_in(jax.random.fold_in(stream_key, 6), dim), (blocks,), jnp.float32, smallest / len(cuts), top_value / len(cuts))
        return jnp.repeat(jnp.exp(steps), dims[dim] // blocks).reshape((-1,) + (1,) * (len(dims) - dim - 1))

    level = one(*cuts[0])
    for cut in cuts[1:]:
        level = level * one(*cut)
    return level


def routed_block(stream_key, own, number, rows, amount, top, bound, lean):
    ranking = jax.random.permutation(stream_key, amount)
    packed, common = load_shares(amount, rows * top, bound, lean, True), load_shares(amount, rows * top, bound, lean, False)
    places = jnp.arange(amount)

    def named(tallies, offset_by):
        used = int((tallies > 0).sum())
        fixed = max(1, used // 4)
        shifted = fixed + (places - fixed + offset_by * (used - fixed)) % max(1, amount - fixed)
        return jnp.zeros((amount,), jnp.int32).at[ranking[jnp.where(places < fixed, places, shifted)]].set(jnp.asarray(tallies, jnp.int32))

    tallies = jnp.where(number % 4 == 0, named(packed, number // 4), named(common, number - number // 4 - 1))
    mixed = jax.random.permutation(jax.random.fold_in(own, 3), amount)
    giver, taker = mixed[0:amount // 2 * 2:2], mixed[1:amount // 2 * 2:2]
    slack = jnp.minimum(tallies[giver] - 1, bound - tallies[taker]) // 2
    slack = jnp.where((giver == ranking[0]) | (taker == ranking[0]) | (tallies[taker] == 0), 0, jnp.maximum(slack, 0))
    shifted = jax.random.randint(jax.random.fold_in(own, 4), (amount // 2,), 0, 1 << 20) % (slack + 1)
    tallies = tallies.at[giver].add(-shifted).at[taker].add(shifted)
    labels = jnp.searchsorted(jnp.cumsum(tallies), jnp.arange(rows * top), side="right").astype(jnp.int32)
    grid = labels.reshape(top, rows).T
    grid = grid[jax.random.permutation(jax.random.fold_in(own, 1), rows)]
    offset_by = jax.random.randint(jax.random.fold_in(own, 2), (rows, 1), 0, top)
    return jnp.take_along_axis(grid, (jnp.arange(top)[None, :] + offset_by) % top, axis=1)


def load_shares(count, total, bound, lean, full):
    loads = [(1 << 20) // math.isqrt(standing ** lean) + 1 for standing in range(1, count + 1)]
    largest = bound if full else min(bound, max(-(-total // count), total * loads[0] // sum(loads)))
    least = 1 if total - largest >= count - 1 else 0
    given, surplus = [largest] + [least] * (count - 1), total - largest - least * (count - 1)
    while surplus > 0:
        free = [i for i in range(1, count) if given[i] < largest] or [i for i in range(1, count) if given[i] < bound]
        mass, left = sum([loads[i] for i in free]), surplus
        for i in free:
            extra = min(bound - given[i], max(1, left * loads[i] // mass), surplus)
            given[i] = given[i] + extra
            surplus = surplus - extra
    return np.array(given)


def gaussian(own_key, extent, deviation, most, shards=(), held_as=jnp.bfloat16):
    loudness = level_of(own_key, extent, shards, -0.22, 0.18) if shards else 1.0
    drawn = jax.random.normal(own_key, extent, jnp.float32) * deviation * loudness
    return jnp.minimum(jnp.maximum(drawn, -most), most).astype(held_as)


def setup_inputs(seed: int = 0) -> dict:
    key_list = jax.random.split(jax.random.key(seed), 14)
    tokens = gaussian(key_list[0], (TOKENS, D), 1.0, 6.0, ((0, 256),))
    norm_gain = jnp.clip(1.0 + 0.18 * jax.random.normal(key_list[1], (D,), jnp.float32), 0.1, 1.9)
    w_query = gaussian(key_list[2], (D, D), D ** -0.5, 0.125, ((1, 4),))
    w_key = gaussian(key_list[3], (D, D), D ** -0.5, 0.125, ((1, 4),))
    w_value = gaussian(key_list[4], (D, D), D ** -0.5, 0.125, ((1, 4),))
    head_gain = jnp.clip(1.0 + 0.18 * jax.random.normal(key_list[5], (D,), jnp.float32), 0.1, 1.9)
    w_out = gaussian(key_list[6], (D, D), D ** -0.5, 0.125, ((0, 4),))
    ffn_gain = jnp.clip(1.0 + 0.18 * jax.random.normal(key_list[7], (D,), jnp.float32), 0.1, 1.9)
    indices_keys = jax.random.split(jax.random.fold_in(key_list[8], 1), TOKENS // TOK_DEV)
    indices_turns = jax.random.permutation(jax.random.fold_in(key_list[8], 3), TOKENS // TOK_DEV)
    indices = jax.vmap(lambda own, number: routed_block(jax.random.fold_in(key_list[8], 2), own, number, TOK_DEV, EXPERTS, 2, CAP, 2))(indices_keys, indices_turns).reshape((TOKENS, 2))
    gates = jnp.clip(0.049804688 + 0.9501953 * jax.random.uniform(key_list[9], (TOKENS, 2), jnp.float32) ** level_of(key_list[9], (TOKENS, 2), ((0, 256),), -0.2, 0.2), 0.049804688, 1.0).astype(jnp.bfloat16)
    w_gate = gaussian(key_list[10], (EXPERTS, D, FF_E), D ** -0.5, 0.125, ((0, 64), (2, 4)))
    w_up = gaussian(key_list[11], (EXPERTS, D, FF_E), D ** -0.5, 0.125, ((0, 64), (2, 4)))
    w_down = gaussian(key_list[12], (EXPERTS, D, FF_E), FF_E ** -0.5, 0.1875, ((0, 64), (2, 4)))
    return dict(tokens=tokens, norm_gain=norm_gain, w_query=w_query, w_key=w_key, w_value=w_value, head_gain=head_gain, w_out=w_out, ffn_gain=ffn_gain, indices=indices, gates=gates, w_gate=w_gate, w_up=w_up, w_down=w_down)


epsilon = 1e-06

def matmul_f32(left, right):
    return jnp.dot(left.astype(jnp.float32), right.astype(jnp.float32), preferred_element_type=jnp.float32)

def rms_rows(values, gain):
    widened = values.astype(jnp.float32)
    mean_square = lax.optimization_barrier(jnp.mean(widened * widened, axis=-1, keepdims=True))
    return widened * lax.rsqrt(mean_square + epsilon) * gain

def rounded(values):
    return lax.optimization_barrier(values.astype(jnp.bfloat16)).astype(jnp.float32)

def block_slots(picked, expert_count, capacity):
    flat_ids = picked.reshape(-1)
    chosen = (flat_ids[:, None] == jnp.arange(expert_count, dtype=jnp.int32)[None, :]).astype(jnp.int32)
    earlier = jnp.cumsum(chosen, axis=0) - chosen
    position = lax.optimization_barrier(jnp.sum(earlier * chosen, axis=1)).astype(jnp.int32)
    return (flat_ids * capacity + position).reshape(picked.shape)

def head_attention(inputs):
    query_head, key_head, value_head = inputs
    block_count = TOKENS // BLK
    causal = jnp.tril(jnp.ones((BLK, BLK), dtype=bool))

    def block_step(kv_state, block):
        query_block, key_block, value_block = block
        score_block = matmul_f32(query_block, key_block.T)
        masked = jnp.where(causal, score_block, 0.0).astype(jnp.bfloat16)
        inside = matmul_f32(masked, value_block)
        carried = jnp.dot(query_block.astype(jnp.float32), kv_state, precision=lax.Precision.HIGHEST)
        kv_state = kv_state + matmul_f32(key_block.T, value_block)
        return (kv_state, inside + carried)
    blocks = (query_head.reshape(block_count, BLK, HD), key_head.reshape(block_count, BLK, HD), value_head.reshape(block_count, BLK, HD))
    final_state, outputs = lax.scan(block_step, jnp.zeros((HD, HD), jnp.float32), blocks)
    return outputs.reshape(TOKENS, HD)

def reference(tokens, norm_gain, w_query, w_key, w_value, head_gain, w_out, ffn_gain, indices, gates, w_gate, w_up, w_down):
    normed = rms_rows(tokens, norm_gain).astype(jnp.bfloat16)
    query = matmul_f32(normed, w_query).astype(jnp.bfloat16)
    key_rows = matmul_f32(normed, w_key).astype(jnp.bfloat16)
    value_rows = matmul_f32(normed, w_value).astype(jnp.bfloat16)

    def by_head(columns):
        return columns.reshape(TOKENS, H, HD).transpose(1, 0, 2)
    attended = lax.map(head_attention, (by_head(query), by_head(key_rows), by_head(value_rows)))
    mean_square = lax.optimization_barrier(jnp.mean(attended * attended, axis=-1, keepdims=True))
    head_out = (attended * lax.rsqrt(mean_square + epsilon) * head_gain.reshape(H, 1, HD)).astype(jnp.bfloat16)
    head_out = head_out.transpose(1, 0, 2).reshape(TOKENS, D)
    group_width = D // N_EXP
    head_total = jnp.zeros((TOKENS, D), jnp.float32)
    for group in range(N_EXP):
        lower = group * group_width
        head_total = head_total + rounded(matmul_f32(head_out[:, lower:lower + group_width], w_out[lower:lower + group_width]))
    residual_rows = (tokens.astype(jnp.float32) + head_total).astype(jnp.bfloat16)
    moe_in = rms_rows(residual_rows, ffn_gain).astype(jnp.bfloat16)
    block_count = TOKENS // TOK_DEV
    picked = indices.reshape(block_count, TOK_DEV, 2)
    slots = jax.vmap(partial(block_slots, expert_count=EXPERTS, capacity=CAP))(picked)
    position = slots - picked * CAP
    column = jnp.arange(block_count, dtype=jnp.int32)[:, None, None] * CAP + position
    token_id = jnp.arange(block_count, dtype=jnp.int32)[:, None, None] * TOK_DEV + jnp.arange(TOK_DEV, dtype=jnp.int32)[None, :, None]
    token_id = jnp.broadcast_to(token_id, picked.shape)
    row_table = jnp.full((EXPERTS, block_count * CAP), TOKENS, jnp.int32).at[picked.reshape(-1), column.reshape(-1)].set(token_id.reshape(-1))
    gate_table = jnp.zeros((EXPERTS, block_count * CAP), jnp.float32).at[picked.reshape(-1), column.reshape(-1)].set(gates.astype(jnp.float32).reshape(-1))
    padded_in = jnp.concatenate([moe_in, jnp.zeros((1, D), jnp.bfloat16)], axis=0)
    hidden_group = FF_E // N_EXP

    def expert_step(total, item):
        row_ids, gate_row, gate_weight, up_weight, down_weight = item
        rows_in = padded_in[row_ids]
        expert_hidden = (jax.nn.silu(matmul_f32(rows_in, gate_weight)) * matmul_f32(rows_in, up_weight)).astype(jnp.bfloat16)
        group_hidden = expert_hidden.reshape(-1, N_EXP, hidden_group).astype(jnp.float32)
        group_down = down_weight.reshape(D, N_EXP, hidden_group).astype(jnp.float32)
        expert_part = jnp.einsum('rgf,dgf->grd', group_hidden, group_down)
        expert_out = lax.optimization_barrier(jnp.sum(rounded(expert_part), axis=0)).astype(jnp.bfloat16)
        total = total.at[row_ids].add(gate_row[:, None] * expert_out.astype(jnp.float32), mode='drop')
        return (total, gate_row[0])
    moe_total, unused_rows = lax.scan(expert_step, jnp.zeros((TOKENS, D), jnp.float32), (row_table, gate_table, w_gate, w_up, w_down))
    return (residual_rows.astype(jnp.float32) + moe_total).astype(jnp.bfloat16)
```

```python
import functools

import jax
import jax.numpy as jnp
from jax import lax
from jax.experimental import pallas as pl
from jax.experimental.pallas import tpu as pltpu
from jax.sharding import PartitionSpec as P

HD = 128
BLK = 512
LANES = 128
MESH = pl.DeviceIdType.MESH


epsilon = 1e-06


def carried_in(array, axis, join, neutral):
    place = lax.axis_index(axis)
    gathered = lax.all_gather(array.astype(jnp.bfloat16), axis)
    state = jnp.zeros_like(array) + jnp.asarray(neutral, array.dtype)

    def one(turn, state):
        return join(state, lax.dynamic_index_in_dim(gathered, turn, 0, False).astype(array.dtype))

    return lax.fori_loop(0, place, one, state)


def rms_rows(values, gain):
    widened = values.astype(jnp.float32)
    mean_square = jnp.mean(widened * widened, axis=-1, keepdims=True)
    return widened * lax.rsqrt(mean_square + epsilon) * gain


def rounded(values):
    return lax.optimization_barrier(values.astype(jnp.bfloat16)).astype(jnp.float32)


def block_slots(picked, expert_count, capacity):
    flat_ids = picked.reshape(-1)
    chosen = (flat_ids[:, None] == jnp.arange(expert_count, dtype=jnp.int32)[None, :]).astype(
        jnp.int32
    )
    earlier = jnp.cumsum(chosen, axis=0) - chosen
    position = jnp.sum(earlier * chosen, axis=1)
    return (flat_ids * capacity + position).reshape(picked.shape)


def add_states(earlier, later):
    return earlier + later


def ctx_grid(count):
    members = 8 if count % 8 == 0 and count > 8 else count // 2
    return count // members, members


def routing(indices, expert_count, capacity, planes, members):
    rows, picks = indices.shape
    flat = indices.reshape(-1)
    count = flat.shape[0]
    number = jnp.arange(count, dtype=jnp.int32)
    same = (flat[:, None] == flat[None, :]) & (number[None, :] < number[:, None])
    position = jnp.sum(same.astype(jnp.int32), axis=1)
    away = jnp.mod(lax.axis_index("ctx") // members - flat // members + planes, planes)
    turn = jnp.where(
        away == 0, 0, jnp.where(away <= planes // 2, 2 * away - 1, 2 * (planes - away))
    )
    slot_of = (turn * members + flat % members) * capacity + position
    slot_ids = jnp.arange(expert_count * capacity, dtype=jnp.int32)
    token_of = jnp.sum(
        jnp.where(slot_ids[:, None] == slot_of[None, :], (number // picks)[None, :], 0), axis=1
    )
    return slot_of.astype(jnp.int32), token_of.astype(jnp.int32)


def relative_order(planes):
    order = [0]
    for far in range(1, planes // 2 + 1):
        order.append(far)
        if len(order) < planes:
            order.append(planes - far)
    return order


def expert_kernel(
    planes,
    members,
    ring,
    capacity,
    moe_ref,
    resid_ref,
    token_ref,
    slot_ref,
    gate_ref,
    wg_hbm,
    wu_hbm,
    wd_hbm,
    wdall_hbm,
    out_ref,
    sent,
    got,
    rows,
    hidden_out,
    hidden_in,
    answer,
    back,
    wgu,
    wd,
    local_sem,
    weight_sem,
    out_sem,
    in_sem,
    ring_send,
    ring_recv,
    hid_send,
    hid_recv,
    ret_send,
    ret_recv,
):
    here = lax.axis_index("ctx")
    y = lax.axis_index("exp")
    z, m = here // members, here % members
    right, left, across = (y + 1) % ring, (y + ring - 1) % ring, (y + 2) % ring
    cell = capacity
    plane_rows = members * cell
    chunk_rows = 2 * plane_rows
    chunks = planes // 2
    order = relative_order(planes)
    half = wgu.shape[0] // 2
    width = wg_hbm.shape[1]

    loads = [
        pltpu.make_async_copy(wg_hbm, wgu.at[:, pl.ds(0, width)], weight_sem.at[0]),
        pltpu.make_async_copy(wu_hbm, wgu.at[:, pl.ds(width, width)], weight_sem.at[1]),
        pltpu.make_async_copy(wd_hbm, wd.at[y], weight_sem.at[2]),
    ]
    for step in range(1, ring):
        other = (y + step) % ring
        loads.append(
            pltpu.make_async_copy(wdall_hbm.at[other], wd.at[other], weight_sem.at[2 + step])
        )
    for load in loads:
        load.start()

    barrier = pltpu.get_barrier_semaphore()
    everyone = planes * members

    def greet(step, carry):
        pl.semaphore_signal(
            barrier, inc=1, device_id=((here + step) % everyone, y), device_id_type=MESH
        )
        return carry

    lax.fori_loop(1, everyone, greet, 0)
    for step in range(1, ring):
        pl.semaphore_signal(
            barrier, inc=1, device_id=(here, (y + step) % ring), device_id_type=MESH
        )

    def pick(slot, carry):
        sent[slot] = moe_ref[token_ref[slot]]
        return carry

    def to_plane(k):
        def one(step, carry):
            t = (m + step) % members
            pltpu.make_async_remote_copy(
                src_ref=sent.at[pl.ds(k * plane_rows + t * cell, cell)],
                dst_ref=got.at[pl.ds(k * plane_rows + m * cell, cell)],
                send_sem=out_sem,
                recv_sem=in_sem.at[k // 2],
                device_id=(((z + planes - order[k]) % planes) * members + t, y),
                device_id_type=MESH,
            ).start()
            return carry

        return one

    for k in range(planes):
        lax.fori_loop(k * plane_rows, (k + 1) * plane_rows, pick, 0, unroll=8)
        if k == 0:
            pl.semaphore_wait(barrier, everyone - 1 + ring - 1)
            own = pl.ds(m * cell, cell)
            pltpu.make_async_copy(sent.at[own], got.at[own], in_sem.at[0]).start()
            lax.fori_loop(1, members, to_plane(k), 0)
        else:
            lax.fori_loop(0, members, to_plane(k), 0)

    def ring_copy(owner, c, columns, target, kind):
        piece = rows.at[owner, pl.ds(c * chunk_rows, chunk_rows), columns]
        return pltpu.make_async_remote_copy(
            src_ref=piece,
            dst_ref=piece,
            send_sem=ring_send.at[kind, c],
            recv_sem=ring_recv.at[kind, c],
            device_id=(here, target),
            device_id_type=MESH,
        )

    everything, low, high = pl.ds(0, 2 * half), pl.ds(0, half), pl.ds(half, half)

    def own_chunk(c):
        part = pl.ds(c * chunk_rows, chunk_rows)
        pltpu.make_async_copy(got.at[part], got.at[part], in_sem.at[c]).wait()
        rows[y, part, :] = got[part].reshape(chunk_rows, 2 * half)
        ring_copy(y, c, everything, right, 0).start()
        ring_copy(y, c, everything, left, 1).start()

    def pass_on(c):
        ring_copy(left, c, everything, right, 0).wait_recv()
        ring_copy(left, c, low, right, 2).start()
        ring_copy(right, c, everything, left, 1).wait_recv()
        ring_copy(right, c, high, left, 3).start()

    def hidden_copy(c, target):
        step = lax.rem(target - y + ring, ring)
        return pltpu.make_async_remote_copy(
            src_ref=hidden_out.at[c, target],
            dst_ref=hidden_in.at[c, y],
            send_sem=hid_send.at[c, step],
            recv_sem=hid_recv.at[c, step],
            device_id=(here, target),
            device_id_type=MESH,
        )

    def hidden_arrival(c, source):
        step = lax.rem(y - source + ring, ring)
        return pltpu.make_async_remote_copy(
            src_ref=hidden_out.at[c, source],
            dst_ref=hidden_in.at[c, source],
            send_sem=hid_send.at[c, step],
            recv_sem=hid_recv.at[c, step],
            device_id=(here, source),
            device_id_type=MESH,
        )

    def expand(c):
        ring_copy(across, c, low, right, 2).wait_recv()
        ring_copy(across, c, high, left, 3).wait_recv()
        part = pl.ds(c * chunk_rows, chunk_rows)
        block = rows[:, part, :].reshape(ring * chunk_rows, 2 * half)
        both = jnp.dot(block, wgu[...], preferred_element_type=jnp.float32)
        gate_rows, up_rows = both[:, :width], both[:, width:]
        hidden = (gate_rows / (1.0 + jnp.exp(-gate_rows)) * up_rows).astype(jnp.bfloat16)
        hidden_out[c] = hidden.reshape(ring, chunk_rows, width)
        for step in range(1, ring):
            hidden_copy(c, (y + step) % ring).start()
        hidden_in[c, y] = hidden_out[c, y]

    def contract(c):
        for step in range(1, ring):
            hidden_arrival(c, (y + step) % ring).wait_recv()
        total = None
        for g in range(ring):
            term = lax.dot_general(
                hidden_in[c, g],
                wd[g],
                (((1,), (1,)), ((), ())),
                preferred_element_type=jnp.float32,
            )
            total = term if total is None else total + term
        part = pl.ds(c * chunk_rows, chunk_rows)
        answer[part] = total.astype(jnp.bfloat16).reshape(chunk_rows, *answer.shape[1:])
        for k in (2 * c, 2 * c + 1):

            def one(step, carry):
                t = (m + step) % members
                pltpu.make_async_remote_copy(
                    src_ref=answer.at[pl.ds(k * plane_rows + t * cell, cell)],
                    dst_ref=back.at[pl.ds(k * plane_rows + m * cell, cell)],
                    send_sem=ret_send,
                    recv_sem=ret_recv,
                    device_id=(((z + order[k]) % planes) * members + t, y),
                    device_id_type=MESH,
                ).start()
                return carry

            if k == 0:
                own = pl.ds(m * cell, cell)
                pltpu.make_async_copy(answer.at[own], back.at[own], ret_recv).start()
                lax.fori_loop(1, members, one, 0)
            else:
                lax.fori_loop(0, members, one, 0)

    for c in range(chunks + 3):
        if c < chunks:
            own_chunk(c)
        if 0 <= c - 1 < chunks:
            pass_on(c - 1)
        if c - 2 == 0:
            loads[0].wait()
            loads[1].wait()
        if 0 <= c - 2 < chunks:
            expand(c - 2)
        if c - 3 == 0:
            for load in loads[2:]:
                load.wait()
        if 0 <= c - 3 < chunks:
            contract(c - 3)

    total_rows = planes * plane_rows
    pltpu.make_async_copy(back, back, ret_recv).wait()

    def blend(t, carry):
        mixed = (
            resid_ref[t].astype(jnp.float32)
            + gate_ref[2 * t] * back[slot_ref[2 * t]].astype(jnp.float32)
            + gate_ref[2 * t + 1] * back[slot_ref[2 * t + 1]].astype(jnp.float32)
        )
        out_ref[t] = mixed.astype(jnp.bfloat16)
        return carry

    lax.fori_loop(0, out_ref.shape[0], blend, 0, unroll=4)

    sent_away = pl.ds(0, total_rows - cell)
    pltpu.make_async_copy(sent.at[sent_away], sent.at[sent_away], out_sem).wait()
    pltpu.make_async_copy(answer.at[sent_away], answer.at[sent_away], ret_send).wait()
    for c in range(chunks):
        ring_copy(y, c, everything, right, 0).wait_send()
        ring_copy(y, c, everything, left, 1).wait_send()
        ring_copy(left, c, low, right, 2).wait_send()
        ring_copy(right, c, high, left, 3).wait_send()
        for step in range(1, ring):
            hidden_copy(c, (y + step) % ring).wait_send()


def expert_layer(moe_tiles, resid_tiles, token_of, slot_of, gates, w_gate, w_up, w_down, wd_all):
    ring = lax.axis_size("exp")
    planes, members = ctx_grid(lax.axis_size("ctx"))
    slots = token_of.shape[0]
    cell = slots // (planes * members)
    groups, lanes = moe_tiles.shape[1:]
    model_width = groups * lanes
    hidden = w_gate.shape[1]
    chunks, chunk_rows = planes // 2, 2 * members * cell
    vmem, smem, anywhere = (
        pl.BlockSpec(memory_space=pltpu.VMEM),
        pl.BlockSpec(memory_space=pltpu.SMEM),
        pl.BlockSpec(memory_space=pl.ANY),
    )
    tiles = pltpu.VMEM((slots, groups, lanes), jnp.bfloat16)
    dma = pltpu.SemaphoreType.DMA
    return pl.pallas_call(
        functools.partial(expert_kernel, planes, members, ring, cell),
        out_shape=jax.ShapeDtypeStruct(moe_tiles.shape, jnp.bfloat16),
        in_specs=[vmem, vmem, smem, smem, smem, anywhere, anywhere, anywhere, anywhere],
        out_specs=vmem,
        scratch_shapes=[
            tiles,
            tiles,
            pltpu.VMEM((ring, slots, model_width), jnp.bfloat16),
            pltpu.VMEM((chunks, ring, chunk_rows, hidden), jnp.bfloat16),
            pltpu.VMEM((chunks, ring, chunk_rows, hidden), jnp.bfloat16),
            tiles,
            tiles,
            pltpu.VMEM((model_width, 2 * hidden), jnp.bfloat16),
            pltpu.VMEM((ring, model_width, hidden), jnp.bfloat16),
            dma((1,)),
            dma((2 + ring,)),
            dma,
            dma((chunks,)),
            dma((4, chunks)),
            dma((4, chunks)),
            dma((chunks, ring)),
            dma((chunks, ring)),
            dma,
            dma,
        ],
        compiler_params=pltpu.CompilerParams(
            collective_id=2, has_side_effects=True, vmem_limit_bytes=60 * 1024 * 1024
        ),
        name="experts",
    )(moe_tiles, resid_tiles, token_of, slot_of, gates, w_gate, w_up, w_down, wd_all)


def on_device(
    tokens,
    norm_gain,
    w_query,
    w_key,
    w_value,
    head_gain,
    w_out,
    ffn_gain,
    indices,
    gates,
    w_gate,
    w_up,
    w_down,
):
    tok_rows, model_width = tokens.shape
    ctx_count = lax.axis_size("ctx")
    local_experts = w_gate.shape[0]
    expert_count = local_experts * ctx_count
    capacity = max(2, (5 * tok_rows + 2 * expert_count - 1) // (2 * expert_count))
    normed = rms_rows(tokens, norm_gain).astype(jnp.bfloat16)
    joined_weights = jnp.concatenate([w_query, w_key, w_value], axis=1)
    projected = jnp.dot(
        lax.all_gather(normed, "exp", axis=0, tiled=True),
        joined_weights,
        preferred_element_type=jnp.float32,
    ).astype(jnp.bfloat16)
    shard_rows = projected.shape[0]
    local_width = w_query.shape[1]
    local_heads = local_width // HD
    block_count = shard_rows // BLK

    def split_heads(columns):
        return columns.reshape(block_count, BLK, local_heads, HD).transpose(0, 2, 1, 3)

    query_blocks = split_heads(projected[:, :local_width])
    key_blocks = split_heads(projected[:, local_width : 2 * local_width])
    value_blocks = split_heads(projected[:, 2 * local_width :])
    causal = jnp.tril(jnp.ones((BLK, BLK), dtype=bool))

    def block_step(kv_state, block):
        query_block, key_block, value_block = block
        score_block = jnp.einsum(
            "hqd,hkd->hqk", query_block, key_block, preferred_element_type=jnp.float32
        )
        masked = jnp.where(causal[None], score_block, 0.0).astype(jnp.bfloat16)
        inside = jnp.einsum("hqk,hkd->hqd", masked, value_block, preferred_element_type=jnp.float32)
        carried = jnp.einsum(
            "hqd,hde->hqe",
            query_block.astype(jnp.float32),
            kv_state,
            precision=lax.Precision.HIGHEST,
        )
        kv_state = kv_state + jnp.einsum(
            "hkd,hke->hde", key_block, value_block, preferred_element_type=jnp.float32
        )
        return (kv_state, inside + carried)

    local_state, inside_rows = lax.scan(
        block_step,
        jnp.zeros((local_heads, HD, HD), jnp.float32),
        (query_blocks, key_blocks, value_blocks),
    )
    before = carried_in(local_state, "ctx", add_states, jnp.zeros_like(local_state))
    carried_rows = jnp.einsum(
        "bhqd,hde->bhqe", query_blocks.astype(jnp.float32), before, precision=lax.Precision.HIGHEST
    )
    attended = inside_rows + carried_rows
    mean_square = jnp.mean(attended * attended, axis=-1, keepdims=True)
    head_out = (
        attended * lax.rsqrt(mean_square + epsilon) * head_gain.reshape(1, local_heads, 1, HD)
    ).astype(jnp.bfloat16)
    head_rows = head_out.transpose(0, 2, 1, 3).reshape(shard_rows, local_width)
    part = head_rows
    head_total = lax.psum_scatter(
        rounded(jnp.dot(part, w_out, preferred_element_type=jnp.float32)).astype(jnp.bfloat16),
        "exp",
        scatter_dimension=0,
        tiled=True,
    ).astype(jnp.float32)
    residual_rows = (tokens.astype(jnp.float32) + head_total).astype(jnp.bfloat16)
    moe_in = rms_rows(residual_rows, ffn_gain).astype(jnp.bfloat16)
    planes, members = ctx_grid(ctx_count)
    slot_of, token_of = routing(indices, expert_count, capacity, planes, members)
    tile = (tok_rows, model_width // LANES, LANES)
    wd_all = lax.all_gather(w_down[0], "exp", axis=0)
    mixed = expert_layer(
        moe_in.reshape(tile),
        residual_rows.reshape(tile),
        token_of,
        slot_of,
        gates.reshape(-1).astype(jnp.float32),
        w_gate[0],
        w_up[0],
        w_down[0],
        wd_all,
    )
    return mixed.reshape(tok_rows, model_width)


def solution(mesh):
    placed = (
        P(("ctx", "exp"), None),
        P(),
        P(None, "exp"),
        P(None, "exp"),
        P(None, "exp"),
        P("exp"),
        P("exp", None),
        P(),
        P(("ctx", "exp"), None),
        P(("ctx", "exp"), None),
        P("ctx", None, "exp"),
        P("ctx", None, "exp"),
        P("ctx", None, "exp"),
    )
    return jax.shard_map(
        on_device, mesh=mesh, in_specs=placed, out_specs=P(("ctx", "exp"), None), check_vma=False
    )
```

```python
import functools

import jax
import jax.numpy as jnp
from jax import lax
from jax.experimental import pallas as pl
from jax.experimental.pallas import tpu as pltpu
from jax.sharding import PartitionSpec as P

HD = 128
LANES = 128
MESH = pl.DeviceIdType.MESH


epsilon = 1e-06


def rms_rows(values, gain):
    widened = values.astype(jnp.float32)
    mean_square = jnp.mean(widened * widened, axis=-1, keepdims=True)
    return widened * lax.rsqrt(mean_square + epsilon) * gain


def ctx_grid(count):
    members = 8 if count % 8 == 0 and count > 8 else count // 2
    return count // members, members


def routing(indices, expert_count, capacity, planes, members):
    rows, picks = indices.shape
    flat = indices.reshape(-1)
    count = flat.shape[0]
    number = jnp.arange(count, dtype=jnp.int32)
    same = (flat[:, None] == flat[None, :]) & (number[None, :] < number[:, None])
    position = jnp.sum(same.astype(jnp.int32), axis=1)
    away = jnp.mod(lax.axis_index("ctx") // members - flat // members + planes, planes)
    turn = jnp.where(
        away == 0, 0, jnp.where(away <= planes // 2, 2 * away - 1, 2 * (planes - away))
    )
    slot_of = (turn * members + flat % members) * capacity + position
    slot_ids = jnp.arange(expert_count * capacity, dtype=jnp.int32)
    token_of = jnp.sum(
        jnp.where(slot_ids[:, None] == slot_of[None, :], (number // picks)[None, :], 0), axis=1
    )
    return slot_of.astype(jnp.int32), token_of.astype(jnp.int32)


def relative_order(planes):
    order = [0]
    for far in range(1, planes // 2 + 1):
        order.append(far)
        if len(order) < planes:
            order.append(planes - far)
    return order


def expert_kernel(
    planes,
    members,
    ring,
    capacity,
    moe_ref,
    resid_ref,
    token_ref,
    slot_ref,
    gate_ref,
    wg_hbm,
    wu_hbm,
    wd_hbm,
    near_hbm,
    out_ref,
    sent,
    got,
    rows,
    hidden_out,
    hidden_in,
    answer,
    back,
    wgu,
    wd,
    weight_sem,
    out_sem,
    in_sem,
    ring_send,
    ring_recv,
    hid_send,
    hid_recv,
    ret_send,
    ret_recv,
    far_send,
    far_recv,
):
    here = lax.axis_index("ctx")
    y = lax.axis_index("exp")
    z, m = here // members, here % members
    right, left, across = (y + 1) % ring, (y + ring - 1) % ring, (y + 2) % ring
    cell = capacity
    plane_rows = members * cell
    chunk_rows = 2 * plane_rows
    chunks = planes // 2
    order = relative_order(planes)
    half = wgu.shape[0] // 2
    width = wg_hbm.shape[1]

    loads = [
        pltpu.make_async_copy(wg_hbm, wgu.at[:, pl.ds(0, width)], weight_sem.at[0]),
        pltpu.make_async_copy(wu_hbm, wgu.at[:, pl.ds(width, width)], weight_sem.at[1]),
        pltpu.make_async_copy(wd_hbm, wd.at[y], weight_sem.at[2]),
    ]
    for side, other in enumerate((left, right)):
        loads.append(
            pltpu.make_async_copy(near_hbm.at[side], wd.at[other], weight_sem.at[3 + side])
        )
    for load in loads:
        load.start()

    barrier = pltpu.get_barrier_semaphore()
    everyone = planes * members

    def greet(step, carry):
        pl.semaphore_signal(
            barrier, inc=1, device_id=((here + step) % everyone, y), device_id_type=MESH
        )
        return carry

    lax.fori_loop(1, everyone, greet, 0)
    for step in range(1, ring):
        pl.semaphore_signal(
            barrier, inc=1, device_id=(here, (y + step) % ring), device_id_type=MESH
        )

    def far_copy(side):
        owner, target = ((left, right), (right, left))[side]
        part = pl.ds(side * half, half)
        return pltpu.make_async_remote_copy(
            src_ref=near_hbm.at[side, part],
            dst_ref=wd.at[owner, part],
            send_sem=far_send.at[side],
            recv_sem=far_recv.at[side],
            device_id=(here, target),
            device_id_type=MESH,
        )

    def pick(slot, carry):
        sent[slot] = moe_ref[token_ref[slot]]
        return carry

    def to_plane(k):
        def one(step, carry):
            t = (m + step) % members
            pltpu.make_async_remote_copy(
                src_ref=sent.at[pl.ds(k * plane_rows + t * cell, cell)],
                dst_ref=got.at[pl.ds(k * plane_rows + m * cell, cell)],
                send_sem=out_sem,
                recv_sem=in_sem.at[k // 2],
                device_id=(((z + planes - order[k]) % planes) * members + t, y),
                device_id_type=MESH,
            ).start()
            return carry

        return one

    for k in range(planes):
        lax.fori_loop(k * plane_rows, (k + 1) * plane_rows, pick, 0, unroll=8)
        if k == 0:
            pl.semaphore_wait(barrier, everyone - 1 + ring - 1)
            far_copy(0).start()
            far_copy(1).start()
            own = pl.ds(m * cell, cell)
            pltpu.make_async_copy(sent.at[own], got.at[own], in_sem.at[0]).start()
            lax.fori_loop(1, members, to_plane(k), 0)
        else:
            lax.fori_loop(0, members, to_plane(k), 0)

    def ring_copy(owner, c, columns, target, kind):
        piece = rows.at[owner, pl.ds(c * chunk_rows, chunk_rows), columns]
        return pltpu.make_async_remote_copy(
            src_ref=piece,
            dst_ref=piece,
            send_sem=ring_send.at[kind, c],
            recv_sem=ring_recv.at[kind, c],
            device_id=(here, target),
            device_id_type=MESH,
        )

    everything, low, high = pl.ds(0, 2 * half), pl.ds(0, half), pl.ds(half, half)

    def own_chunk(c):
        part = pl.ds(c * chunk_rows, chunk_rows)
        pltpu.make_async_copy(got.at[part], got.at[part], in_sem.at[c]).wait()
        rows[y, part, :] = got[part].reshape(chunk_rows, 2 * half)
        ring_copy(y, c, everything, right, 0).start()
        ring_copy(y, c, everything, left, 1).start()

    def pass_on(c):
        ring_copy(left, c, everything, right, 0).wait_recv()
        ring_copy(left, c, low, right, 2).start()
        ring_copy(right, c, everything, left, 1).wait_recv()
        ring_copy(right, c, high, left, 3).start()

    def hidden_copy(c, target):
        step = lax.rem(target - y + ring, ring)
        return pltpu.make_async_remote_copy(
            src_ref=hidden_out.at[c, target],
            dst_ref=hidden_in.at[c, y],
            send_sem=hid_send.at[c, step],
            recv_sem=hid_recv.at[c, step],
            device_id=(here, target),
            device_id_type=MESH,
        )

    def hidden_arrival(c, source):
        step = lax.rem(y - source + ring, ring)
        return pltpu.make_async_remote_copy(
            src_ref=hidden_out.at[c, source],
            dst_ref=hidden_in.at[c, source],
            send_sem=hid_send.at[c, step],
            recv_sem=hid_recv.at[c, step],
            device_id=(here, source),
            device_id_type=MESH,
        )

    def expand(c):
        ring_copy(across, c, low, right, 2).wait_recv()
        ring_copy(across, c, high, left, 3).wait_recv()
        part = pl.ds(c * chunk_rows, chunk_rows)
        block = rows[:, part, :].reshape(ring * chunk_rows, 2 * half)
        both = jnp.dot(block, wgu[...], preferred_element_type=jnp.float32)
        gate_rows, up_rows = both[:, :width], both[:, width:]
        hidden = (gate_rows / (1.0 + jnp.exp(-gate_rows)) * up_rows).astype(jnp.bfloat16)
        hidden_out[c] = hidden.reshape(ring, chunk_rows, width)
        for step in range(1, ring):
            hidden_copy(c, (y + step) % ring).start()
        hidden_in[c, y] = hidden_out[c, y]

    def contract(c):
        for step in range(1, ring):
            hidden_arrival(c, (y + step) % ring).wait_recv()
        total = None
        for g in range(ring):
            term = lax.dot_general(
                hidden_in[c, g],
                wd[g],
                (((1,), (1,)), ((), ())),
                preferred_element_type=jnp.float32,
            )
            total = term if total is None else total + term
        part = pl.ds(c * chunk_rows, chunk_rows)
        answer[part] = total.astype(jnp.bfloat16).reshape(chunk_rows, *answer.shape[1:])
        for k in (2 * c, 2 * c + 1):

            def one(step, carry):
                t = (m + step) % members
                pltpu.make_async_remote_copy(
                    src_ref=answer.at[pl.ds(k * plane_rows + t * cell, cell)],
                    dst_ref=back.at[pl.ds(k * plane_rows + m * cell, cell)],
                    send_sem=ret_send,
                    recv_sem=ret_recv,
                    device_id=(((z + order[k]) % planes) * members + t, y),
                    device_id_type=MESH,
                ).start()
                return carry

            if k == 0:
                own = pl.ds(m * cell, cell)
                pltpu.make_async_copy(answer.at[own], back.at[own], ret_recv).start()
                lax.fori_loop(1, members, one, 0)
            else:
                lax.fori_loop(0, members, one, 0)

    for c in range(chunks + 3):
        if c < chunks:
            own_chunk(c)
        if 0 <= c - 1 < chunks:
            pass_on(c - 1)
        if c - 2 == 0:
            loads[0].wait()
            loads[1].wait()
        if 0 <= c - 2 < chunks:
            expand(c - 2)
        if c - 3 == 0:
            for load in loads[2:]:
                load.wait()
            far_copy(0).wait_recv()
            far_copy(1).wait_recv()
        if 0 <= c - 3 < chunks:
            contract(c - 3)

    total_rows = planes * plane_rows
    pltpu.make_async_copy(back, back, ret_recv).wait()

    def blend(t, carry):
        mixed = (
            resid_ref[t].astype(jnp.float32)
            + gate_ref[2 * t] * back[slot_ref[2 * t]].astype(jnp.float32)
            + gate_ref[2 * t + 1] * back[slot_ref[2 * t + 1]].astype(jnp.float32)
        )
        out_ref[t] = mixed.astype(jnp.bfloat16)
        return carry

    lax.fori_loop(0, out_ref.shape[0], blend, 0, unroll=4)

    far_copy(0).wait_send()
    far_copy(1).wait_send()
    sent_away = pl.ds(0, total_rows - cell)
    pltpu.make_async_copy(sent.at[sent_away], sent.at[sent_away], out_sem).wait()
    pltpu.make_async_copy(answer.at[sent_away], answer.at[sent_away], ret_send).wait()
    for c in range(chunks):
        ring_copy(y, c, everything, right, 0).wait_send()
        ring_copy(y, c, everything, left, 1).wait_send()
        ring_copy(left, c, low, right, 2).wait_send()
        ring_copy(right, c, high, left, 3).wait_send()
        for step in range(1, ring):
            hidden_copy(c, (y + step) % ring).wait_send()


def expert_layer(moe_tiles, resid_tiles, token_of, slot_of, gates, w_gate, w_up, w_down, near):
    ring = lax.axis_size("exp")
    planes, members = ctx_grid(lax.axis_size("ctx"))
    slots = token_of.shape[0]
    cell = slots // (planes * members)
    groups, lanes = moe_tiles.shape[1:]
    model_width = groups * lanes
    hidden = w_gate.shape[1]
    chunks, chunk_rows = planes // 2, 2 * members * cell
    vmem, smem, anywhere = (
        pl.BlockSpec(memory_space=pltpu.VMEM),
        pl.BlockSpec(memory_space=pltpu.SMEM),
        pl.BlockSpec(memory_space=pl.ANY),
    )
    tiles = pltpu.VMEM((slots, groups, lanes), jnp.bfloat16)
    dma = pltpu.SemaphoreType.DMA
    return pl.pallas_call(
        functools.partial(expert_kernel, planes, members, ring, cell),
        out_shape=jax.ShapeDtypeStruct(moe_tiles.shape, jnp.bfloat16),
        in_specs=[vmem, vmem, smem, smem, smem, anywhere, anywhere, anywhere, anywhere],
        out_specs=vmem,
        scratch_shapes=[
            tiles,
            tiles,
            pltpu.VMEM((ring, slots, model_width), jnp.bfloat16),
            pltpu.VMEM((chunks, ring, chunk_rows, hidden), jnp.bfloat16),
            pltpu.VMEM((chunks, ring, chunk_rows, hidden), jnp.bfloat16),
            tiles,
            tiles,
            pltpu.VMEM((model_width, 2 * hidden), jnp.bfloat16),
            pltpu.VMEM((ring, model_width, hidden), jnp.bfloat16),
            dma((5,)),
            dma,
            dma((chunks,)),
            dma((4, chunks)),
            dma((4, chunks)),
            dma((chunks, ring)),
            dma((chunks, ring)),
            dma,
            dma,
            dma((2,)),
            dma((2,)),
        ],
        compiler_params=pltpu.CompilerParams(
            collective_id=2, has_side_effects=True, vmem_limit_bytes=60 * 1024 * 1024
        ),
        name="experts",
    )(moe_tiles, resid_tiles, token_of, slot_of, gates, w_gate, w_up, w_down, near)


def attention_kernel(
    planes,
    members,
    ring,
    tokens_ref,
    norm_gain_ref,
    head_gain_ref,
    ffn_gain_ref,
    wq_hbm,
    wk_hbm,
    wv_hbm,
    wo_hbm,
    wd_hbm,
    moe_ref,
    resid_ref,
    near_hbm,
    wqkv,
    wo,
    normed,
    qkv,
    state,
    plane_states,
    plane_total,
    totals,
    earlier_out,
    earlier,
    inside,
    heads,
    parts,
    via,
    landed,
    weight_sem,
    ring_send,
    ring_recv,
    near_send,
    near_recv,
    scan_send,
    scan_recv,
    part_send,
    part_recv,
):
    here = lax.axis_index("ctx")
    y = lax.axis_index("exp")
    z, m = here // members, here % members
    right, left, across = (y + 1) % ring, (y + ring - 1) % ring, (y + 2) % ring
    rows, model_width = tokens_ref.shape
    width = wq_hbm.shape[1]
    local_heads = width // HD
    block = ring * rows
    piece = state.shape[1]
    per_head = HD // piece

    loads = [
        pltpu.make_async_copy(w, wqkv.at[:, pl.ds(i * width, width)], weight_sem.at[i])
        for i, w in enumerate((wq_hbm, wk_hbm, wv_hbm))
    ]
    loads.append(pltpu.make_async_copy(wo_hbm, wo, weight_sem.at[3]))
    for load in loads:
        load.start()

    barrier = pltpu.get_barrier_semaphore()
    for step in range(1, ring):
        pl.semaphore_signal(
            barrier, inc=1, device_id=(here, (y + step) % ring), device_id_type=MESH
        )

    def plane_mate(step):
        return (m + step) % members

    def greet_mate(step, carry):
        pl.semaphore_signal(
            barrier, inc=1, device_id=(z * members + plane_mate(step), y), device_id_type=MESH
        )
        return carry

    def greet_plane(step, carry):
        pl.semaphore_signal(
            barrier,
            inc=1,
            device_id=(((z + step) % planes) * members + m, y),
            device_id_type=MESH,
        )
        return carry

    lax.fori_loop(1, members, greet_mate, 0)
    lax.fori_loop(1, planes, greet_plane, 0)

    normed[y] = rms_rows(tokens_ref[...], norm_gain_ref[...]).astype(jnp.bfloat16)
    pl.semaphore_wait(barrier, ring - 1 + members - 1 + planes - 1)

    low, high = pl.ds(0, rows // 2), pl.ds(rows // 2, rows // 2)

    def ring_copy(owner, part, target, kind):
        return pltpu.make_async_remote_copy(
            src_ref=normed.at[owner, part],
            dst_ref=normed.at[owner, part],
            send_sem=ring_send.at[kind],
            recv_sem=ring_recv.at[kind],
            device_id=(here, target),
            device_id_type=MESH,
        )

    ring_copy(y, low, right, 0).start()
    ring_copy(y, high, left, 1).start()
    ring_copy(y, high, right, 2).start()
    ring_copy(y, low, left, 3).start()

    def near_copy(target, kind):
        return pltpu.make_async_remote_copy(
            src_ref=wd_hbm,
            dst_ref=near_hbm.at[kind],
            send_sem=near_send.at[kind],
            recv_sem=near_recv.at[kind],
            device_id=(here, target),
            device_id_type=MESH,
        )

    def project(owner):
        qkv[owner] = jnp.dot(
            normed[owner], wqkv[...], preferred_element_type=jnp.float32
        ).astype(jnp.bfloat16)

    for load in loads[:3]:
        load.wait()
    project(y)
    ring_copy(left, low, right, 0).wait_recv()
    ring_copy(left, low, right, 4).start()
    ring_copy(right, high, left, 1).wait_recv()
    ring_copy(right, high, left, 5).start()
    near_copy(right, 0).start()
    near_copy(left, 1).start()
    ring_copy(left, high, right, 2).wait_recv()
    project(left)
    ring_copy(right, low, left, 3).wait_recv()
    project(right)
    ring_copy(across, low, right, 4).wait_recv()
    ring_copy(across, high, left, 5).wait_recv()
    project(across)

    def columns(kind, head):
        return pl.ds(kind * width + head * HD, HD)

    for head in range(local_heads):
        head_state = lax.dot_general(
            qkv[:, :, columns(1, head)].reshape(block, HD),
            qkv[:, :, columns(2, head)].reshape(block, HD),
            (((0,), (0,)), ((), ())),
            preferred_element_type=jnp.float32,
        )
        state[head * per_head : (head + 1) * per_head] = head_state.astype(jnp.bfloat16).reshape(
            per_head, piece, HD
        )

    def to_mates(source, landing, kind):
        def one(step, carry):
            t = plane_mate(step)
            pltpu.make_async_remote_copy(
                src_ref=source.at[t],
                dst_ref=landing.at[m],
                send_sem=scan_send.at[kind],
                recv_sem=scan_recv.at[kind],
                device_id=(z * members + t, y),
                device_id_type=MESH,
            ).start()
            return carry

        lax.fori_loop(1, members, one, 0)

    def all_of(buffer, count, semaphore):
        part = buffer.at[pl.ds(0, count)]
        pltpu.make_async_copy(part, part, semaphore).wait()

    def within(head):
        tall = block // 2
        keys = qkv[:, :, columns(1, head)].reshape(block, HD)
        values = qkv[:, :, columns(2, head)].reshape(block, HD)
        queries = qkv[:, :, columns(0, head)].reshape(block, HD)
        for i in range(2):
            reach = (i + 1) * tall
            scores = lax.dot_general(
                queries[i * tall : reach],
                keys[:reach],
                (((1,), (1,)), ((), ())),
                preferred_element_type=jnp.float32,
            )
            at = lax.broadcasted_iota(jnp.int32, (tall, reach), 0) + i * tall
            of = lax.broadcasted_iota(jnp.int32, (tall, reach), 1)
            masked = jnp.where(of <= at, scores, 0.0).astype(jnp.bfloat16)
            inside[head, i * tall : reach] = jnp.dot(
                masked, values[:reach], preferred_element_type=jnp.float32
            )

    to_mates(state, plane_states, 0)
    plane_states[m] = state[m]
    within(0)
    all_of(plane_states, members - 1, scan_recv.at[0])
    running = jnp.zeros((piece, HD), jnp.float32)
    before = []
    for t in range(members):
        before.append(running)
        running = running + plane_states[t].astype(jnp.float32)
    plane_total[...] = running.astype(jnp.bfloat16)

    def to_planes(step, carry):
        pltpu.make_async_remote_copy(
            src_ref=plane_total,
            dst_ref=totals.at[z],
            send_sem=scan_send.at[1],
            recv_sem=scan_recv.at[1],
            device_id=(((z + step) % planes) * members + m, y),
            device_id_type=MESH,
        ).start()
        return carry

    lax.fori_loop(1, planes, to_planes, 0)
    totals[z] = plane_total[...]
    within(1)
    within(2)
    all_of(totals, planes - 1, scan_recv.at[1])
    base = jnp.zeros((piece, HD), jnp.float32)
    for other in range(planes):
        base = base + jnp.where(other < z, totals[other].astype(jnp.float32), 0.0)
    for t in range(members):
        earlier_out[t] = (base + before[t]).astype(jnp.bfloat16)
    to_mates(earlier_out, earlier, 2)
    earlier[m] = earlier_out[m]
    within(3)
    all_of(earlier, members - 1, scan_recv.at[2])

    for head in range(local_heads):
        carried = jnp.dot(
            qkv[:, :, columns(0, head)].reshape(block, HD),
            earlier[head * per_head : (head + 1) * per_head].reshape(HD, HD),
            preferred_element_type=jnp.float32,
        )
        gain = head_gain_ref[:, head * HD : (head + 1) * HD]
        heads[:, :, head * HD : (head + 1) * HD] = (
            rms_rows(inside[head] + carried, gain).astype(jnp.bfloat16).reshape(ring, rows, HD)
        )

    def share(target):
        return jnp.dot(heads[target], wo[...], preferred_element_type=jnp.float32).astype(
            jnp.bfloat16
        )

    def part_copy(source, landing, target, kind):
        return pltpu.make_async_remote_copy(
            src_ref=source,
            dst_ref=landing,
            send_sem=part_send.at[kind],
            recv_sem=part_recv.at[kind],
            device_id=(here, target),
            device_id_type=MESH,
        )

    def part_send_of(kind):
        source, landing, target = (
            (parts.at[0, low], via.at[0], right),
            (parts.at[0, high], via.at[1], left),
            (parts.at[1, high], landed.at[0, high], right),
            (parts.at[2, low], landed.at[1, low], left),
            (parts.at[1, low], landed.at[0, low], right),
            (parts.at[2, high], landed.at[1, high], left),
        )[kind]
        return part_copy(source, landing, target, kind)

    loads[3].wait()
    parts[0] = share(across)
    part_send_of(0).start()
    part_send_of(1).start()
    parts[1] = share(right)
    part_send_of(2).start()
    parts[2] = share(left)
    part_send_of(3).start()
    part_send_of(0).wait_recv()
    parts[1, low] = (
        parts[1, low].astype(jnp.float32) + via[0].astype(jnp.float32)
    ).astype(jnp.bfloat16)
    part_send_of(4).start()
    part_send_of(1).wait_recv()
    parts[2, high] = (
        parts[2, high].astype(jnp.float32) + via[1].astype(jnp.float32)
    ).astype(jnp.bfloat16)
    part_send_of(5).start()
    total = tokens_ref[...].astype(jnp.float32) + share(y).astype(jnp.float32)
    for kind in range(2, 6):
        part_send_of(kind).wait_recv()
    residual = (
        total + landed[0].astype(jnp.float32) + landed[1].astype(jnp.float32)
    ).astype(jnp.bfloat16)
    resid_ref[...] = residual.reshape(resid_ref.shape)
    moe_ref[...] = (
        rms_rows(residual, ffn_gain_ref[...]).astype(jnp.bfloat16).reshape(moe_ref.shape)
    )

    near_copy(right, 0).wait()
    near_copy(left, 1).wait()
    ring_copy(y, low, right, 0).wait_send()
    ring_copy(y, high, left, 1).wait_send()
    ring_copy(y, high, right, 2).wait_send()
    ring_copy(y, low, left, 3).wait_send()
    ring_copy(left, low, right, 4).wait_send()
    ring_copy(right, high, left, 5).wait_send()
    all_of(state, members - 1, scan_send.at[0])
    all_of(totals, planes - 1, scan_send.at[1])
    all_of(earlier_out, members - 1, scan_send.at[2])
    for kind in range(6):
        part_send_of(kind).wait_send()


def attention_layer(
    tokens, norm_gain, w_query, w_key, w_value, head_gain, w_out, ffn_gain, w_down
):
    ring = lax.axis_size("exp")
    planes, members = ctx_grid(lax.axis_size("ctx"))
    rows, model_width = tokens.shape
    width = w_query.shape[1]
    block = ring * rows
    piece = width // members
    vmem, anywhere = pl.BlockSpec(memory_space=pltpu.VMEM), pl.BlockSpec(memory_space=pl.ANY)
    tile = jax.ShapeDtypeStruct((rows, model_width // LANES, LANES), jnp.bfloat16)
    dma = pltpu.SemaphoreType.DMA

    def half(*shape):
        return pltpu.VMEM(shape, jnp.bfloat16)

    return pl.pallas_call(
        functools.partial(attention_kernel, planes, members, ring),
        out_shape=(tile, tile, jax.ShapeDtypeStruct((2, *w_down.shape), jnp.bfloat16)),
        in_specs=[vmem] * 4 + [anywhere] * 5,
        out_specs=(vmem, vmem, anywhere),
        scratch_shapes=[
            half(model_width, 3 * width),
            half(width, model_width),
            half(ring, rows, model_width),
            half(ring, rows, 3 * width),
            half(members, piece, HD),
            half(members, piece, HD),
            half(piece, HD),
            half(planes, piece, HD),
            half(members, piece, HD),
            half(members, piece, HD),
            pltpu.VMEM((width // HD, block, HD), jnp.float32),
            half(ring, rows, width),
            half(3, rows, model_width),
            half(2, rows // 2, model_width),
            half(2, rows, model_width),
            dma((4,)),
            dma((6,)),
            dma((6,)),
            dma((2,)),
            dma((2,)),
            dma((3,)),
            dma((3,)),
            dma((6,)),
            dma((6,)),
        ],
        compiler_params=pltpu.CompilerParams(
            collective_id=1, has_side_effects=True, vmem_limit_bytes=60 * 1024 * 1024
        ),
        name="attention",
    )(
        tokens,
        norm_gain.reshape(1, -1),
        head_gain.reshape(1, -1),
        ffn_gain.reshape(1, -1),
        w_query,
        w_key,
        w_value,
        w_out,
        w_down,
    )


def on_device(
    tokens,
    norm_gain,
    w_query,
    w_key,
    w_value,
    head_gain,
    w_out,
    ffn_gain,
    indices,
    gates,
    w_gate,
    w_up,
    w_down,
):
    tok_rows, model_width = tokens.shape
    ctx_count = lax.axis_size("ctx")
    expert_count = w_gate.shape[0] * ctx_count
    capacity = max(2, (5 * tok_rows + 2 * expert_count - 1) // (2 * expert_count))
    planes, members = ctx_grid(ctx_count)
    slot_of, token_of = routing(indices, expert_count, capacity, planes, members)
    moe_tiles, resid_tiles, near = attention_layer(
        tokens, norm_gain, w_query, w_key, w_value, head_gain, w_out, ffn_gain, w_down[0]
    )
    mixed = expert_layer(
        moe_tiles,
        resid_tiles,
        token_of,
        slot_of,
        gates.reshape(-1).astype(jnp.float32),
        w_gate[0],
        w_up[0],
        w_down[0],
        near,
    )
    return mixed.reshape(tok_rows, model_width)


def solution(mesh):
    placed = (
        P(("ctx", "exp"), None),
        P(),
        P(None, "exp"),
        P(None, "exp"),
        P(None, "exp"),
        P("exp"),
        P("exp", None),
        P(),
        P(("ctx", "exp"), None),
        P(("ctx", "exp"), None),
        P("ctx", None, "exp"),
        P("ctx", None, "exp"),
        P("ctx", None, "exp"),
    )
    return jax.shard_map(
        on_device, mesh=mesh, in_specs=placed, out_specs=P(("ctx", "exp"), None), check_vma=False
    )
```

```python
import functools

import jax
import jax.numpy as jnp
from jax import lax
from jax.experimental import pallas as pl
from jax.experimental.pallas import tpu as pltpu
from jax.sharding import PartitionSpec as P

HD = 128
LANES = 128
MESH = pl.DeviceIdType.MESH


epsilon = 1e-06


def rms_rows(values, gain):
    widened = values.astype(jnp.float32)
    mean_square = jnp.mean(widened * widened, axis=-1, keepdims=True)
    return widened * lax.rsqrt(mean_square + epsilon) * gain


def ctx_grid(count):
    members = 8 if count % 8 == 0 and count > 8 else count // 2
    return count // members, members


def routing(indices, expert_count, capacity, planes, members):
    rows, picks = indices.shape
    flat = indices.reshape(-1)
    count = flat.shape[0]
    number = jnp.arange(count, dtype=jnp.int32)
    same = (flat[:, None] == flat[None, :]) & (number[None, :] < number[:, None])
    position = jnp.sum(same.astype(jnp.int32), axis=1)
    away = jnp.mod(lax.axis_index("ctx") // members - flat // members + planes, planes)
    turn = jnp.where(
        away == 0, 0, jnp.where(away <= planes // 2, 2 * away - 1, 2 * (planes - away))
    )
    turn = planes - 1 - turn
    slot_of = (turn * members + flat % members) * capacity + position
    slot_ids = jnp.arange(expert_count * capacity, dtype=jnp.int32)
    token_of = jnp.sum(
        jnp.where(slot_ids[:, None] == slot_of[None, :], (number // picks)[None, :], 0), axis=1
    )
    return slot_of.astype(jnp.int32), token_of.astype(jnp.int32)


def relative_order(planes):
    order = [0]
    for far in range(1, planes // 2 + 1):
        order.append(far)
        if len(order) < planes:
            order.append(planes - far)
    return order[::-1]


def expert_kernel(
    planes,
    members,
    ring,
    capacity,
    moe_ref,
    resid_ref,
    token_ref,
    slot_ref,
    gate_ref,
    wg_hbm,
    wu_hbm,
    wd_hbm,
    near_hbm,
    out_ref,
    sent,
    got,
    rows,
    hidden_out,
    hidden_in,
    answer,
    back,
    wgu,
    wd,
    weight_sem,
    out_sem,
    in_sem,
    ring_send,
    ring_recv,
    hid_send,
    hid_recv,
    ret_send,
    ret_recv,
    far_send,
    far_recv,
):
    here = lax.axis_index("ctx")
    y = lax.axis_index("exp")
    z, m = here // members, here % members
    right, left, across = (y + 1) % ring, (y + ring - 1) % ring, (y + 2) % ring
    cell = capacity
    plane_rows = members * cell
    chunk_rows = 2 * plane_rows
    chunks = planes // 2
    order = relative_order(planes)
    half = wgu.shape[0] // 2
    width = wg_hbm.shape[1]

    loads = [
        pltpu.make_async_copy(wg_hbm, wgu.at[:, pl.ds(0, width)], weight_sem.at[0]),
        pltpu.make_async_copy(wu_hbm, wgu.at[:, pl.ds(width, width)], weight_sem.at[1]),
        pltpu.make_async_copy(wd_hbm, wd.at[y], weight_sem.at[2]),
    ]
    for side, other in enumerate((left, right)):
        loads.append(
            pltpu.make_async_copy(near_hbm.at[side], wd.at[other], weight_sem.at[3 + side])
        )
    for load in loads:
        load.start()

    barrier = pltpu.get_barrier_semaphore()
    everyone = planes * members

    def greet(step, carry):
        pl.semaphore_signal(
            barrier, inc=1, device_id=((here + step) % everyone, y), device_id_type=MESH
        )
        return carry

    lax.fori_loop(1, everyone, greet, 0)
    for step in range(1, ring):
        pl.semaphore_signal(
            barrier, inc=1, device_id=(here, (y + step) % ring), device_id_type=MESH
        )

    def far_copy(side):
        owner, target = ((left, right), (right, left))[side]
        part = pl.ds(side * half, half)
        return pltpu.make_async_remote_copy(
            src_ref=near_hbm.at[side, part],
            dst_ref=wd.at[owner, part],
            send_sem=far_send.at[side],
            recv_sem=far_recv.at[side],
            device_id=(here, target),
            device_id_type=MESH,
        )

    def pick(slot, carry):
        sent[slot] = moe_ref[token_ref[slot]]
        return carry

    def to_plane(k):
        def one(step, carry):
            t = (m + step) % members
            pltpu.make_async_remote_copy(
                src_ref=sent.at[pl.ds(k * plane_rows + t * cell, cell)],
                dst_ref=got.at[pl.ds(k * plane_rows + m * cell, cell)],
                send_sem=out_sem,
                recv_sem=in_sem.at[k // 2],
                device_id=(((z + planes - order[k]) % planes) * members + t, y),
                device_id_type=MESH,
            ).start()
            return carry

        return one

    for k in range(planes):
        lax.fori_loop(k * plane_rows, (k + 1) * plane_rows, pick, 0, unroll=8)
        if k == 0:
            pl.semaphore_wait(barrier, everyone - 1 + ring - 1)
            far_copy(0).start()
            far_copy(1).start()
        if order[k] == 0:
            own = pl.ds(k * plane_rows + m * cell, cell)
            pltpu.make_async_copy(sent.at[own], got.at[own], in_sem.at[k // 2]).start()
            lax.fori_loop(1, members, to_plane(k), 0)
        else:
            lax.fori_loop(0, members, to_plane(k), 0)

    def ring_copy(owner, c, columns, target, kind):
        piece = rows.at[owner, pl.ds(c * chunk_rows, chunk_rows), columns]
        return pltpu.make_async_remote_copy(
            src_ref=piece,
            dst_ref=piece,
            send_sem=ring_send.at[kind, c],
            recv_sem=ring_recv.at[kind, c],
            device_id=(here, target),
            device_id_type=MESH,
        )

    everything, low, high = pl.ds(0, 2 * half), pl.ds(0, half), pl.ds(half, half)

    def own_chunk(c):
        part = pl.ds(c * chunk_rows, chunk_rows)
        pltpu.make_async_copy(got.at[part], got.at[part], in_sem.at[c]).wait()
        rows[y, part, :] = got[part].reshape(chunk_rows, 2 * half)
        ring_copy(y, c, everything, right, 0).start()
        ring_copy(y, c, everything, left, 1).start()

    def pass_on(c):
        ring_copy(left, c, everything, right, 0).wait_recv()
        ring_copy(left, c, low, right, 2).start()
        ring_copy(right, c, everything, left, 1).wait_recv()
        ring_copy(right, c, high, left, 3).start()

    def hidden_copy(c, target):
        step = lax.rem(target - y + ring, ring)
        return pltpu.make_async_remote_copy(
            src_ref=hidden_out.at[c, target],
            dst_ref=hidden_in.at[c, y],
            send_sem=hid_send.at[c, step],
            recv_sem=hid_recv.at[c, step],
            device_id=(here, target),
            device_id_type=MESH,
        )

    def hidden_arrival(c, source):
        step = lax.rem(y - source + ring, ring)
        return pltpu.make_async_remote_copy(
            src_ref=hidden_out.at[c, source],
            dst_ref=hidden_in.at[c, source],
            send_sem=hid_send.at[c, step],
            recv_sem=hid_recv.at[c, step],
            device_id=(here, source),
            device_id_type=MESH,
        )

    def expand(c):
        ring_copy(across, c, low, right, 2).wait_recv()
        ring_copy(across, c, high, left, 3).wait_recv()
        part = pl.ds(c * chunk_rows, chunk_rows)
        block = rows[:, part, :].reshape(ring * chunk_rows, 2 * half)
        both = jnp.dot(block, wgu[...], preferred_element_type=jnp.float32)
        gate_rows, up_rows = both[:, :width], both[:, width:]
        hidden = (gate_rows / (1.0 + jnp.exp(-gate_rows)) * up_rows).astype(jnp.bfloat16)
        hidden_out[c] = hidden.reshape(ring, chunk_rows, width)
        for step in range(1, ring):
            hidden_copy(c, (y + step) % ring).start()
        hidden_in[c, y] = hidden_out[c, y]

    def contract(c):
        for step in range(1, ring):
            hidden_arrival(c, (y + step) % ring).wait_recv()
        total = None
        for g in range(ring):
            term = lax.dot_general(
                hidden_in[c, g],
                wd[g],
                (((1,), (1,)), ((), ())),
                preferred_element_type=jnp.float32,
            )
            total = term if total is None else total + term
        part = pl.ds(c * chunk_rows, chunk_rows)
        answer[part] = total.astype(jnp.bfloat16).reshape(chunk_rows, *answer.shape[1:])
        for k in (2 * c, 2 * c + 1):

            def one(step, carry):
                t = (m + step) % members
                pltpu.make_async_remote_copy(
                    src_ref=answer.at[pl.ds(k * plane_rows + t * cell, cell)],
                    dst_ref=back.at[pl.ds(k * plane_rows + m * cell, cell)],
                    send_sem=ret_send,
                    recv_sem=ret_recv,
                    device_id=(((z + order[k]) % planes) * members + t, y),
                    device_id_type=MESH,
                ).start()
                return carry

            if order[k] == 0:
                own = pl.ds(k * plane_rows + m * cell, cell)
                pltpu.make_async_copy(answer.at[own], back.at[own], ret_recv).start()
                lax.fori_loop(1, members, one, 0)
            else:
                lax.fori_loop(0, members, one, 0)

    for c in range(chunks + 3):
        if c < chunks:
            own_chunk(c)
        if 0 <= c - 1 < chunks:
            pass_on(c - 1)
        if c - 2 == 0:
            loads[0].wait()
            loads[1].wait()
        if 0 <= c - 2 < chunks:
            expand(c - 2)
        if c - 3 == 0:
            for load in loads[2:]:
                load.wait()
            far_copy(0).wait_recv()
            far_copy(1).wait_recv()
        if 0 <= c - 3 < chunks:
            contract(c - 3)

    total_rows = planes * plane_rows
    pltpu.make_async_copy(back, back, ret_recv).wait()

    def blend(t, carry):
        mixed = (
            resid_ref[t].astype(jnp.float32)
            + gate_ref[2 * t] * back[slot_ref[2 * t]].astype(jnp.float32)
            + gate_ref[2 * t + 1] * back[slot_ref[2 * t + 1]].astype(jnp.float32)
        )
        out_ref[t] = mixed.astype(jnp.bfloat16)
        return carry

    lax.fori_loop(0, out_ref.shape[0], blend, 0, unroll=4)

    far_copy(0).wait_send()
    far_copy(1).wait_send()
    sent_away = pl.ds(0, total_rows - cell)
    pltpu.make_async_copy(sent.at[sent_away], sent.at[sent_away], out_sem).wait()
    pltpu.make_async_copy(answer.at[sent_away], answer.at[sent_away], ret_send).wait()
    for c in range(chunks):
        ring_copy(y, c, everything, right, 0).wait_send()
        ring_copy(y, c, everything, left, 1).wait_send()
        ring_copy(left, c, low, right, 2).wait_send()
        ring_copy(right, c, high, left, 3).wait_send()
        for step in range(1, ring):
            hidden_copy(c, (y + step) % ring).wait_send()


def expert_layer(moe_tiles, resid_tiles, token_of, slot_of, gates, w_gate, w_up, w_down, near):
    ring = lax.axis_size("exp")
    planes, members = ctx_grid(lax.axis_size("ctx"))
    slots = token_of.shape[0]
    cell = slots // (planes * members)
    groups, lanes = moe_tiles.shape[1:]
    model_width = groups * lanes
    hidden = w_gate.shape[1]
    chunks, chunk_rows = planes // 2, 2 * members * cell
    vmem, smem, anywhere = (
        pl.BlockSpec(memory_space=pltpu.VMEM),
        pl.BlockSpec(memory_space=pltpu.SMEM),
        pl.BlockSpec(memory_space=pl.ANY),
    )
    tiles = pltpu.VMEM((slots, groups, lanes), jnp.bfloat16)
    dma = pltpu.SemaphoreType.DMA
    return pl.pallas_call(
        functools.partial(expert_kernel, planes, members, ring, cell),
        out_shape=jax.ShapeDtypeStruct(moe_tiles.shape, jnp.bfloat16),
        in_specs=[vmem, vmem, smem, smem, smem, anywhere, anywhere, anywhere, anywhere],
        out_specs=vmem,
        scratch_shapes=[
            tiles,
            tiles,
            pltpu.VMEM((ring, slots, model_width), jnp.bfloat16),
            pltpu.VMEM((chunks, ring, chunk_rows, hidden), jnp.bfloat16),
            pltpu.VMEM((chunks, ring, chunk_rows, hidden), jnp.bfloat16),
            tiles,
            tiles,
            pltpu.VMEM((model_width, 2 * hidden), jnp.bfloat16),
            pltpu.VMEM((ring, model_width, hidden), jnp.bfloat16),
            dma((5,)),
            dma,
            dma((chunks,)),
            dma((4, chunks)),
            dma((4, chunks)),
            dma((chunks, ring)),
            dma((chunks, ring)),
            dma,
            dma,
            dma((2,)),
            dma((2,)),
        ],
        compiler_params=pltpu.CompilerParams(
            collective_id=2, has_side_effects=True, vmem_limit_bytes=60 * 1024 * 1024
        ),
        name="experts",
    )(moe_tiles, resid_tiles, token_of, slot_of, gates, w_gate, w_up, w_down, near)


def attention_kernel(
    planes,
    members,
    ring,
    tokens_ref,
    norm_gain_ref,
    head_gain_ref,
    ffn_gain_ref,
    wq_hbm,
    wk_hbm,
    wv_hbm,
    wo_hbm,
    wd_hbm,
    moe_ref,
    resid_ref,
    near_hbm,
    wqkv,
    wo,
    normed,
    qkv,
    state,
    plane_states,
    plane_total,
    totals,
    earlier_out,
    earlier,
    inside,
    heads,
    parts,
    via,
    landed,
    weight_sem,
    ring_send,
    ring_recv,
    near_send,
    near_recv,
    scan_send,
    scan_recv,
    part_send,
    part_recv,
):
    here = lax.axis_index("ctx")
    y = lax.axis_index("exp")
    z, m = here // members, here % members
    right, left, across = (y + 1) % ring, (y + ring - 1) % ring, (y + 2) % ring
    rows, model_width = tokens_ref.shape
    width = wq_hbm.shape[1]
    local_heads = width // HD
    block = ring * rows
    piece = state.shape[1]
    per_head = HD // piece

    loads = [
        pltpu.make_async_copy(w, wqkv.at[:, pl.ds(i * width, width)], weight_sem.at[i])
        for i, w in enumerate((wq_hbm, wk_hbm, wv_hbm))
    ]
    loads.append(pltpu.make_async_copy(wo_hbm, wo, weight_sem.at[3]))
    for load in loads:
        load.start()

    barrier = pltpu.get_barrier_semaphore()
    for step in range(1, ring):
        pl.semaphore_signal(
            barrier, inc=1, device_id=(here, (y + step) % ring), device_id_type=MESH
        )

    def plane_mate(step):
        return (m + step) % members

    def greet_mate(step, carry):
        pl.semaphore_signal(
            barrier, inc=1, device_id=(z * members + plane_mate(step), y), device_id_type=MESH
        )
        return carry

    def greet_plane(step, carry):
        pl.semaphore_signal(
            barrier,
            inc=1,
            device_id=(((z + step) % planes) * members + m, y),
            device_id_type=MESH,
        )
        return carry

    lax.fori_loop(1, members, greet_mate, 0)
    lax.fori_loop(1, planes, greet_plane, 0)

    normed[y] = rms_rows(tokens_ref[...], norm_gain_ref[...]).astype(jnp.bfloat16)
    pl.semaphore_wait(barrier, ring - 1 + members - 1 + planes - 1)

    low, high = pl.ds(0, rows // 2), pl.ds(rows // 2, rows // 2)

    def ring_copy(owner, part, target, kind):
        return pltpu.make_async_remote_copy(
            src_ref=normed.at[owner, part],
            dst_ref=normed.at[owner, part],
            send_sem=ring_send.at[kind],
            recv_sem=ring_recv.at[kind],
            device_id=(here, target),
            device_id_type=MESH,
        )

    ring_copy(y, low, right, 0).start()
    ring_copy(y, high, left, 1).start()
    ring_copy(y, high, right, 2).start()
    ring_copy(y, low, left, 3).start()

    def near_copy(target, kind):
        return pltpu.make_async_remote_copy(
            src_ref=wd_hbm,
            dst_ref=near_hbm.at[kind],
            send_sem=near_send.at[kind],
            recv_sem=near_recv.at[kind],
            device_id=(here, target),
            device_id_type=MESH,
        )

    def project(owner):
        qkv[owner] = jnp.dot(
            normed[owner], wqkv[...], preferred_element_type=jnp.float32
        ).astype(jnp.bfloat16)

    for load in loads[:3]:
        load.wait()
    project(y)
    ring_copy(left, low, right, 0).wait_recv()
    ring_copy(left, low, right, 4).start()
    ring_copy(right, high, left, 1).wait_recv()
    ring_copy(right, high, left, 5).start()
    near_copy(right, 0).start()
    near_copy(left, 1).start()
    ring_copy(left, high, right, 2).wait_recv()
    project(left)
    ring_copy(right, low, left, 3).wait_recv()
    project(right)
    ring_copy(across, low, right, 4).wait_recv()
    ring_copy(across, high, left, 5).wait_recv()
    project(across)

    def columns(kind, head):
        return pl.ds(kind * width + head * HD, HD)

    for head in range(local_heads):
        head_state = lax.dot_general(
            qkv[:, :, columns(1, head)].reshape(block, HD),
            qkv[:, :, columns(2, head)].reshape(block, HD),
            (((0,), (0,)), ((), ())),
            preferred_element_type=jnp.float32,
        )
        state[head * per_head : (head + 1) * per_head] = head_state.astype(jnp.bfloat16).reshape(
            per_head, piece, HD
        )

    def to_mates(source, landing, kind):
        def one(step, carry):
            t = plane_mate(step)
            pltpu.make_async_remote_copy(
                src_ref=source.at[t],
                dst_ref=landing.at[m],
                send_sem=scan_send.at[kind],
                recv_sem=scan_recv.at[kind],
                device_id=(z * members + t, y),
                device_id_type=MESH,
            ).start()
            return carry

        lax.fori_loop(1, members, one, 0)

    def all_of(buffer, count, semaphore):
        part = buffer.at[pl.ds(0, count)]
        pltpu.make_async_copy(part, part, semaphore).wait()

    def within(head):
        tall = block // 2
        keys = qkv[:, :, columns(1, head)].reshape(block, HD)
        values = qkv[:, :, columns(2, head)].reshape(block, HD)
        queries = qkv[:, :, columns(0, head)].reshape(block, HD)
        for i in range(2):
            reach = (i + 1) * tall
            scores = lax.dot_general(
                queries[i * tall : reach],
                keys[:reach],
                (((1,), (1,)), ((), ())),
                preferred_element_type=jnp.float32,
            )
            at = lax.broadcasted_iota(jnp.int32, (tall, reach), 0) + i * tall
            of = lax.broadcasted_iota(jnp.int32, (tall, reach), 1)
            masked = jnp.where(of <= at, scores, 0.0).astype(jnp.bfloat16)
            inside[head, i * tall : reach] = jnp.dot(
                masked, values[:reach], preferred_element_type=jnp.float32
            )

    to_mates(state, plane_states, 0)
    plane_states[m] = state[m]
    within(0)
    all_of(plane_states, members - 1, scan_recv.at[0])
    running = jnp.zeros((piece, HD), jnp.float32)
    before = []
    for t in range(members):
        before.append(running)
        running = running + plane_states[t].astype(jnp.float32)
    plane_total[...] = running.astype(jnp.bfloat16)

    def to_planes(step, carry):
        pltpu.make_async_remote_copy(
            src_ref=plane_total,
            dst_ref=totals.at[z],
            send_sem=scan_send.at[1],
            recv_sem=scan_recv.at[1],
            device_id=(((z + step) % planes) * members + m, y),
            device_id_type=MESH,
        ).start()
        return carry

    lax.fori_loop(1, planes, to_planes, 0)
    totals[z] = plane_total[...]
    within(1)
    within(2)
    all_of(totals, planes - 1, scan_recv.at[1])
    base = jnp.zeros((piece, HD), jnp.float32)
    for other in range(planes):
        base = base + jnp.where(other < z, totals[other].astype(jnp.float32), 0.0)
    for t in range(members):
        earlier_out[t] = (base + before[t]).astype(jnp.bfloat16)
    to_mates(earlier_out, earlier, 2)
    earlier[m] = earlier_out[m]
    within(3)
    all_of(earlier, members - 1, scan_recv.at[2])

    for head in range(local_heads):
        carried = jnp.dot(
            qkv[:, :, columns(0, head)].reshape(block, HD),
            earlier[head * per_head : (head + 1) * per_head].reshape(HD, HD),
            preferred_element_type=jnp.float32,
        )
        gain = head_gain_ref[:, head * HD : (head + 1) * HD]
        heads[:, :, head * HD : (head + 1) * HD] = (
            rms_rows(inside[head] + carried, gain).astype(jnp.bfloat16).reshape(ring, rows, HD)
        )

    def share(target):
        return jnp.dot(heads[target], wo[...], preferred_element_type=jnp.float32).astype(
            jnp.bfloat16
        )

    def part_copy(source, landing, target, kind):
        return pltpu.make_async_remote_copy(
            src_ref=source,
            dst_ref=landing,
            send_sem=part_send.at[kind],
            recv_sem=part_recv.at[kind],
            device_id=(here, target),
            device_id_type=MESH,
        )

    def part_send_of(kind):
        source, landing, target = (
            (parts.at[0, low], via.at[0], right),
            (parts.at[0, high], via.at[1], left),
            (parts.at[1, high], landed.at[0, high], right),
            (parts.at[2, low], landed.at[1, low], left),
            (parts.at[1, low], landed.at[0, low], right),
            (parts.at[2, high], landed.at[1, high], left),
        )[kind]
        return part_copy(source, landing, target, kind)

    loads[3].wait()
    parts[0] = share(across)
    part_send_of(0).start()
    part_send_of(1).start()
    parts[1] = share(right)
    part_send_of(2).start()
    parts[2] = share(left)
    part_send_of(3).start()
    part_send_of(0).wait_recv()
    parts[1, low] = (
        parts[1, low].astype(jnp.float32) + via[0].astype(jnp.float32)
    ).astype(jnp.bfloat16)
    part_send_of(4).start()
    part_send_of(1).wait_recv()
    parts[2, high] = (
        parts[2, high].astype(jnp.float32) + via[1].astype(jnp.float32)
    ).astype(jnp.bfloat16)
    part_send_of(5).start()
    total = tokens_ref[...].astype(jnp.float32) + share(y).astype(jnp.float32)
    for kind in range(2, 6):
        part_send_of(kind).wait_recv()
    residual = (
        total + landed[0].astype(jnp.float32) + landed[1].astype(jnp.float32)
    ).astype(jnp.bfloat16)
    resid_ref[...] = residual.reshape(resid_ref.shape)
    moe_ref[...] = (
        rms_rows(residual, ffn_gain_ref[...]).astype(jnp.bfloat16).reshape(moe_ref.shape)
    )

    near_copy(right, 0).wait()
    near_copy(left, 1).wait()
    ring_copy(y, low, right, 0).wait_send()
    ring_copy(y, high, left, 1).wait_send()
    ring_copy(y, high, right, 2).wait_send()
    ring_copy(y, low, left, 3).wait_send()
    ring_copy(left, low, right, 4).wait_send()
    ring_copy(right, high, left, 5).wait_send()
    all_of(state, members - 1, scan_send.at[0])
    all_of(totals, planes - 1, scan_send.at[1])
    all_of(earlier_out, members - 1, scan_send.at[2])
    for kind in range(6):
        part_send_of(kind).wait_send()


def attention_layer(
    tokens, norm_gain, w_query, w_key, w_value, head_gain, w_out, ffn_gain, w_down
):
    ring = lax.axis_size("exp")
    planes, members = ctx_grid(lax.axis_size("ctx"))
    rows, model_width = tokens.shape
    width = w_query.shape[1]
    block = ring * rows
    piece = width // members
    vmem, anywhere = pl.BlockSpec(memory_space=pltpu.VMEM), pl.BlockSpec(memory_space=pl.ANY)
    tile = jax.ShapeDtypeStruct((rows, model_width // LANES, LANES), jnp.bfloat16)
    dma = pltpu.SemaphoreType.DMA

    def half(*shape):
        return pltpu.VMEM(shape, jnp.bfloat16)

    return pl.pallas_call(
        functools.partial(attention_kernel, planes, members, ring),
        out_shape=(tile, tile, jax.ShapeDtypeStruct((2, *w_down.shape), jnp.bfloat16)),
        in_specs=[vmem] * 4 + [anywhere] * 5,
        out_specs=(vmem, vmem, anywhere),
        scratch_shapes=[
            half(model_width, 3 * width),
            half(width, model_width),
            half(ring, rows, model_width),
            half(ring, rows, 3 * width),
            half(members, piece, HD),
            half(members, piece, HD),
            half(piece, HD),
            half(planes, piece, HD),
            half(members, piece, HD),
            half(members, piece, HD),
            pltpu.VMEM((width // HD, block, HD), jnp.float32),
            half(ring, rows, width),
            half(3, rows, model_width),
            half(2, rows // 2, model_width),
            half(2, rows, model_width),
            dma((4,)),
            dma((6,)),
            dma((6,)),
            dma((2,)),
            dma((2,)),
            dma((3,)),
            dma((3,)),
            dma((6,)),
            dma((6,)),
        ],
        compiler_params=pltpu.CompilerParams(
            collective_id=1, has_side_effects=True, vmem_limit_bytes=60 * 1024 * 1024
        ),
        name="attention",
    )(
        tokens,
        norm_gain.reshape(1, -1),
        head_gain.reshape(1, -1),
        ffn_gain.reshape(1, -1),
        w_query,
        w_key,
        w_value,
        w_out,
        w_down,
    )


def on_device(
    tokens,
    norm_gain,
    w_query,
    w_key,
    w_value,
    head_gain,
    w_out,
    ffn_gain,
    indices,
    gates,
    w_gate,
    w_up,
    w_down,
):
    tok_rows, model_width = tokens.shape
    ctx_count = lax.axis_size("ctx")
    expert_count = w_gate.shape[0] * ctx_count
    capacity = max(2, (5 * tok_rows + 2 * expert_count - 1) // (2 * expert_count))
    planes, members = ctx_grid(ctx_count)
    slot_of, token_of = routing(indices, expert_count, capacity, planes, members)
    moe_tiles, resid_tiles, near = attention_layer(
        tokens, norm_gain, w_query, w_key, w_value, head_gain, w_out, ffn_gain, w_down[0]
    )
    mixed = expert_layer(
        moe_tiles,
        resid_tiles,
        token_of,
        slot_of,
        gates.reshape(-1).astype(jnp.float32),
        w_gate[0],
        w_up[0],
        w_down[0],
        near,
    )
    return mixed.reshape(tok_rows, model_width)


def solution(mesh):
    placed = (
        P(("ctx", "exp"), None),
        P(),
        P(None, "exp"),
        P(None, "exp"),
        P(None, "exp"),
        P("exp"),
        P("exp", None),
        P(),
        P(("ctx", "exp"), None),
        P(("ctx", "exp"), None),
        P("ctx", None, "exp"),
        P("ctx", None, "exp"),
        P("ctx", None, "exp"),
    )
    return jax.shard_map(
        on_device, mesh=mesh, in_specs=placed, out_specs=P(("ctx", "exp"), None), check_vma=False
    )
```
